32 devices in a mesh: dp: 2 (over core), ctx: 16 (over z, y, x).
Axes of the slice: x: 2, y: 2, z: 4, core: 2. Of those that a mesh axis runs over, the one named last changes fastest.
Arguments:
- layer_input: bfloat16 [2, 2048, 16384], P('dp', 'ctx'), may hold values from -6 to 6
- query_rows: bfloat16 [2, 2048, 1024], P('dp', 'ctx'), may hold values from -512 to 512
- key_rows: bfloat16 [2, 2048, 128], P('dp', 'ctx'), may hold values from -5 to 5
- value_rows: bfloat16 [2, 2048, 128], P('dp', 'ctx'), may hold values from -6 to 6
- out_grad: bfloat16 [2, 2048, 1024], P('dp', 'ctx'), may hold values from -6 to 6
- block_order: int32 [32], replicated, may hold values from 0 to 31, each once
- master: float32 [16384, 1280], P(('dp', 'ctx')), may hold values from -3 to 3
- moment_one: float32 [16384, 1280], P(('dp', 'ctx')), may hold values from -6 to 6
- moment_two: float32 [16384, 1280], P(('dp', 'ctx')), may hold values from 0.5 to 20
Outputs:
- new_master: float32 [16384, 1280], P(('dp', 'ctx'))
- new_moment_one: float32 [16384, 1280], P(('dp', 'ctx'))
- new_moment_two: float32 [16384, 1280], P(('dp', 'ctx'))
The draws below stay inside these ranges and needn't reach their ends.
Inputs may be any that keep to these rules, and one draw needn't show every extreme that they name: Stored rows j * 64 to (j + 1) * 64 - 1 of every sequence hold positions block_order[j] * 64 onward, in order; each of the 32 blocks appears once.
All inputs are finite; a program needn't handle non-finite values.
Results may differ from the reference program's by a relative error of at most 0.0048.
Values may be sent and summed in bfloat16 or wider, within the bound.
No kernel may reach another device: no remote copies, remote signals or barrier semaphores. Data moves between devices by JAX's collectives and lax.ppermute only.
A program may use at most 64 MiB of HBM per device.

```python
import math
import jax
import jax.numpy as jnp
from jax import lax

D = 16384
HD = 128
GROUP = 8
STEP = 10
BATCH = 2
LENGTH = 2048
HALF = 64
BLOCKS = 32
QW = 1024
QKV = 1280


def draw_common(key):
    keys_all = jnp.clip(jax.random.normal(jax.random.fold_in(key, 11), (BATCH, LENGTH, HD), jnp.float32), -5.0, 5.0)
    query_all = jnp.clip(jax.random.normal(jax.random.fold_in(key, 12), (BATCH, LENGTH, QW), jnp.float32), -5.0, 5.0)
    return (keys_all, query_all)


def draw_key_rows(key, part):
    return draw_common(key)[0].astype(jnp.bfloat16)


def draw_query_rows(key, part):
    return draw_common(key)[1].astype(jnp.bfloat16)


def steps_of(key, dims, pieces, smallest, high):
    def one(position, parts):
        heights = jax.random.uniform(jax.random.fold_in(jax.random.fold_in(key, 6), position), (parts,), jnp.float32, smallest / len(pieces), high / len(pieces))
        return jnp.repeat(jnp.exp(heights), dims[position] // parts).reshape((-1,) + (1,) * (len(dims) - position - 1))

    loudness = one(*pieces[0])
    for cut in pieces[1:]:
        loudness = loudness * one(*cut)
    return loudness


def gaussian(stream_key, shape, deviation, bound, pieces=(), kind=jnp.bfloat16):
    entries = jax.random.normal(stream_key, shape, jnp.float32) * deviation
    if len(pieces) > 0:
        entries = steps_of(stream_key, shape, pieces, -0.22, 0.18) * entries
    return jnp.clip(entries, min=-bound, max=bound).astype(kind)


def setup_inputs(seed: int = 0) -> dict:
    splits = jax.random.split(jax.random.key(seed), 10)
    layer_input = gaussian(splits[0], (BATCH, LENGTH, D), 1.0, 6.0, ((0, 2), (1, 16)))
    query_rows = draw_query_rows(jax.random.fold_in(splits[9], 71), 0)
    key_rows = draw_key_rows(jax.random.fold_in(splits[9], 71), 0)
    value_rows = gaussian(splits[3], (BATCH, LENGTH, HD), 1.0, 6.0, ((0, 2), (1, 16)))
    out_grad = gaussian(splits[4], (BATCH, LENGTH, QW), 1.0, 6.0, ((0, 2), (1, 16)))
    block_order = jax.random.permutation(splits[5], BLOCKS).astype(jnp.int32)
    master = gaussian(splits[6], (D, QKV), 0.5, 3.0, ((0, 32),), jnp.float32)
    moment_one = gaussian(splits[7], (D, QKV), 1.0, 6.0, ((0, 32),), jnp.float32)
    moment_two = jnp.clip(jnp.exp(math.log(20.0) - 3.6888795 * jax.random.uniform(splits[8], (D, QKV), jnp.float32) ** steps_of(splits[8], (D, QKV), ((0, 32),), -0.2, 0.2)), 0.5, 20.0)
    return {"layer_input": layer_input, "query_rows": query_rows, "key_rows": key_rows, "value_rows": value_rows, "out_grad": out_grad, "block_order": block_order, "master": master, "moment_one": moment_one, "moment_two": moment_two}


NEG_FILL = -1e+30
BETA_ONE = 0.9
BETA_TWO = 0.95
EPSILON = 1e-08
LEARN_RATE = 0.01
DECAY = 0.1

def sequence_grads(query_seq, key_seq, value_seq, grad_seq, pos_all):
    score_scale = 1.0 / math.sqrt(HD)
    row_total = LENGTH * GROUP
    rows_q = query_seq.reshape(row_total, HD)
    rows_o = grad_seq.reshape(row_total, HD)
    query_pos = jnp.repeat(pos_all, GROUP)
    blk_rows = math.gcd(row_total, 2048)

    def advance(carried, block_index):
        key_acc, value_acc = carried
        first_row = (block_index * blk_rows).astype(jnp.int32)
        q_blk = lax.dynamic_slice_in_dim(rows_q, first_row, blk_rows, 0)
        o_blk = lax.dynamic_slice_in_dim(rows_o, first_row, blk_rows, 0)
        qpos_blk = lax.dynamic_slice_in_dim(query_pos, first_row, blk_rows, 0)
        scores = jnp.dot(q_blk, key_seq.T, preferred_element_type=jnp.float32) * score_scale
        visible = pos_all[None, :] <= qpos_blk[:, None]
        row_top = lax.optimization_barrier(jnp.max(jnp.where(visible, scores, NEG_FILL), axis=1))
        denom_sum = lax.optimization_barrier(jnp.sum(jnp.where(visible, jnp.exp(scores - row_top[:, None]), 0.0), axis=1))
        log_total = row_top + jnp.log(denom_sum)
        prob_full = jnp.where(visible, jnp.exp(scores - log_total[:, None]), 0.0)
        grad_prob = jnp.dot(o_blk, value_seq.T, preferred_element_type=jnp.float32)
        delta_row = lax.optimization_barrier(jnp.sum(prob_full * grad_prob, axis=1))
        dscore = (prob_full * (grad_prob - delta_row[:, None]) * score_scale).astype(jnp.bfloat16)
        prob_low = prob_full.astype(jnp.bfloat16)
        query_grad = jnp.dot(dscore, key_seq, preferred_element_type=jnp.float32).astype(jnp.bfloat16)
        key_acc = key_acc + jnp.dot(dscore.T, q_blk, preferred_element_type=jnp.float32)
        value_acc = value_acc + jnp.dot(prob_low.T, o_blk, preferred_element_type=jnp.float32)
        return ((key_acc, value_acc), query_grad)
    empty_acc = jnp.zeros((LENGTH, HD), jnp.float32)
    finals, query_grads = lax.scan(advance, (empty_acc, empty_acc), jnp.arange(row_total // blk_rows, dtype=jnp.int32))
    key_acc, value_acc = finals
    return jnp.concatenate([query_grads.reshape(LENGTH, GROUP * HD), key_acc.astype(jnp.bfloat16), value_acc.astype(jnp.bfloat16)], axis=1)

def reference(layer_input, query_rows, key_rows, value_rows, out_grad, block_order, master, moment_one, moment_two):
    pos_all = (block_order[:, None] * HALF + jnp.arange(HALF, dtype=jnp.int32)[None, :]).reshape(LENGTH).astype(jnp.int32)

    def per_sequence(grad_acc, seq_items):
        x_seq, q_seq, k_seq, v_seq, o_seq = seq_items
        grad_cols = sequence_grads(q_seq, k_seq, v_seq, o_seq, pos_all)
        return (grad_acc + jnp.dot(x_seq.T, grad_cols, preferred_element_type=jnp.float32), None)
    grad_full, unused_out = lax.scan(per_sequence, jnp.zeros((D, QKV), jnp.float32), (layer_input, query_rows, key_rows, value_rows, out_grad))
    new_one = BETA_ONE * moment_one + (1.0 - BETA_ONE) * grad_full
    new_two = BETA_TWO * moment_two + (1.0 - BETA_TWO) * grad_full * grad_full
    corr_one = 1.0 - BETA_ONE ** STEP
    corr_two = 1.0 - BETA_TWO ** STEP
    update = new_one / corr_one / (jnp.sqrt(new_two / corr_two) + EPSILON)
    new_master = master - LEARN_RATE * (update + DECAY * master)
    return (new_master, new_one, new_two)
```

```python
import functools
import math

import jax
import jax.numpy as jnp
from jax import lax
from jax.experimental import pallas as pl
from jax.experimental.pallas import tpu as pltpu
from jax.sharding import PartitionSpec as P


STEP = 10
BETA_ONE = 0.9
BETA_TWO = 0.95
EPSILON = 1e-08
LEARN_RATE = 0.01
DECAY = 0.1
NEG_FILL = -1e30
LOG2E = 1.4426950408889634
ROW_CONTRACT = (((1,), (1,)), ((), ()))
F32 = jnp.float32
BF16 = jnp.bfloat16


def swap(block, mask, count):
    return lax.ppermute(block, "ctx", [(i, i ^ mask) for i in range(count)])


def stage_bits(count):
    bits = []
    bit = count // 2
    while bit >= 4:
        bits.append(bit)
        bit //= 2
    return bits


def slot_order(count):
    order = [0]
    for bit in stage_bits(count):
        order = order + [o ^ bit for o in order]
    return order


def fan_out(held, count, relay=False):
    parts = [held] + [swap(held, j, count) for j in range(1, 3)]
    if not relay:
        return parts + [swap(held, 3, count)]
    half = held.shape[1] // 2
    left = swap(parts[1][:, :half], 2, count)
    right = swap(parts[2][:, half:], 1, count)
    return parts + [(left, right)]


def spread(block, count, relay=False):
    held = block
    for bit in stage_bits(count):
        held = jnp.concatenate([held, swap(held, bit, count)], axis=0)
    return fan_out(held, count, relay)


def total_terms(parts, count):
    total = parts[0].astype(F32)
    for j in range(1, 4):
        other = swap(parts[j], j, count)
        total = total + other.astype(F32)
    tok = total.shape[0] // (count // 4)
    order = slot_order(count)
    for bit in stage_bits(count):
        other = swap(total.astype(BF16), bit, count)
        blocks = [other[order.index(o ^ bit) * tok :][:tok] for o in order]
        total = total + jnp.concatenate(blocks, axis=0).astype(F32)
    return total.astype(BF16)


def pack_kernel(masks, dp_count, ctx_count, me_ref, x_ref, *refs):
    outs = refs[: len(masks)]
    held_ref, sem = refs[len(masks) :]
    own = held_ref.shape[2]
    copies = []
    for i, mask in enumerate(masks):
        for d in range(dp_count):
            first = pl.multiple_of((d * ctx_count + (me_ref[0] ^ mask)) * own, 128)
            at = i * dp_count + d
            copies.append(
                pltpu.make_async_copy(
                    x_ref.at[:, pl.ds(first, own)], held_ref.at[at], sem.at[at]
                )
            )
    for copy in copies:
        copy.start()
    for i, out_ref in enumerate(outs):
        for d in range(dp_count):
            at = i * dp_count + d
            copies[at].wait()
            out_ref[d * own : (d + 1) * own, :] = held_ref[at].T


def pack(rows, me, masks, dp_count, ctx_count, own):
    tok = rows.shape[0]
    count = len(masks)
    if own % 128:
        slabs = rows.T.reshape(dp_count, ctx_count, own, tok).transpose(1, 0, 2, 3)
        slabs = slabs.reshape(ctx_count, dp_count * own, tok)
        return [lax.dynamic_index_in_dim(slabs, me[0] ^ mask, 0, False) for mask in masks]
    return pl.pallas_call(
        functools.partial(pack_kernel, masks, dp_count, ctx_count),
        in_specs=[
            pl.BlockSpec(memory_space=pltpu.SMEM),
            pl.BlockSpec(memory_space=pltpu.HBM),
        ],
        out_specs=[pl.BlockSpec(memory_space=pltpu.VMEM)] * count,
        out_shape=[jax.ShapeDtypeStruct((dp_count * own, tok), rows.dtype)] * count,
        scratch_shapes=[
            pltpu.VMEM((count * dp_count, tok, own), rows.dtype),
            pltpu.SemaphoreType.DMA((count * dp_count,)),
        ],
        compiler_params=pltpu.CompilerParams(vmem_limit_bytes=8 << 20),
        cost_estimate=pl.CostEstimate(
            flops=0, bytes_accessed=4 * count * dp_count * own * tok, transcendentals=0
        ),
        name="pack_rows",
    )(me, pltpu.with_memory_space_constraint(rows, pltpu.HBM))


def attention_kernel(order, me_ref, blocks_ref, q_ref, o_ref, *refs):
    kv_refs = refs[:4]
    dq_ref = refs[4]
    dkv_refs = refs[5:9]
    s_ref, g_ref, kt_ref, acc_ref = refs[9:]
    step = pl.program_id(0)
    tok, pair = q_ref.shape
    head_dim = pair // 2
    half = tok // 2
    rows = kv_refs[0].shape[0]
    me = me_ref[0]
    scale = 1.0 / math.sqrt(head_dim)

    @pl.when(step == 0)
    def _():
        acc_ref[...] = jnp.zeros_like(acc_ref)
        for j in range(4):
            kt_ref[:, j * rows : (j + 1) * rows] = kv_refs[j][:, :head_dim].T

    q2 = jnp.concatenate([q_ref[:, :head_dim], q_ref[:, head_dim:]], axis=0)
    o2 = jnp.concatenate([o_ref[:, :head_dim], o_ref[:, head_dim:]], axis=0)
    lane = lax.broadcasted_iota(jnp.int32, (1, 2 * tok), 1)
    lane = jnp.where(lane >= tok, lane - tok, lane)
    first = blocks_ref[2 * me]
    second = blocks_ref[2 * me + 1]
    query_pos = jnp.where(lane < half, first * half + lane, second * half + lane - half)
    in_block = lax.broadcasted_iota(jnp.int32, (half, 2 * tok), 0)

    top = jnp.full((1, 2 * tok), NEG_FILL, F32)
    for j in range(4):
        scores = lax.dot_general(
            kv_refs[j][:, :head_dim], q2, ROW_CONTRACT, preferred_element_type=F32
        )
        for i, o in enumerate(order):
            for u in range(2):
                lo = i * tok + u * half
                key_base = blocks_ref[2 * (me ^ (o ^ j)) + u] * half
                part = scores[lo : lo + half] * (scale * LOG2E)
                part = jnp.where(in_block <= query_pos - key_base, part, NEG_FILL)
                s_ref[j * rows + lo : j * rows + lo + half, :] = part
                top = jnp.maximum(top, jnp.max(part, axis=0, keepdims=True))
    denom = jnp.zeros((1, 2 * tok), F32)
    inner = jnp.zeros((1, 2 * tok), F32)
    for j in range(4):
        grads = lax.dot_general(
            kv_refs[j][:, head_dim:], o2, ROW_CONTRACT, preferred_element_type=F32
        )
        g_ref[j * rows : (j + 1) * rows, :] = grads
        for lo in range(0, rows, half):
            at = slice(j * rows + lo, j * rows + lo + half)
            weight = jnp.exp2(s_ref[at, :] - top)
            s_ref[at, :] = weight
            denom = denom + jnp.sum(weight, axis=0, keepdims=True)
            inner = inner + jnp.sum(weight * grads[lo : lo + half], axis=0, keepdims=True)
    inv = 1.0 / denom
    delta = inner * inv
    dqt = jnp.zeros((head_dim, 2 * tok), F32)
    for j in range(4):
        at = slice(j * rows, (j + 1) * rows)
        prob = s_ref[at, :] * inv
        ds = (prob * (g_ref[at, :] - delta) * scale).astype(BF16)
        prob = prob.astype(BF16)
        acc_ref[at, :head_dim] += jnp.dot(ds, q2, preferred_element_type=F32)
        acc_ref[at, head_dim:] += jnp.dot(prob, o2, preferred_element_type=F32)
        dqt = dqt + jnp.dot(kt_ref[:, at], ds, preferred_element_type=F32)
    dq2 = dqt.T.astype(BF16)
    dq_ref[:, :head_dim] = dq2[:tok]
    dq_ref[:, head_dim:] = dq2[tok:]

    @pl.when(step == pl.num_programs(0) - 1)
    def _():
        for j in range(4):
            dkv_refs[j][...] = acc_ref[j * rows : (j + 1) * rows, :].astype(BF16)


def attention(me, blocks, q, o, kv_parts, order):
    tok, width = q.shape
    rows, kv_width = kv_parts[0].shape
    head_dim = kv_width // 2
    pair = 2 * head_dim
    flops = 2 * 5 * tok * (width // head_dim) * 4 * rows * head_dim
    row_spec = pl.BlockSpec((tok, pair), lambda g, *_: (0, g))
    kv_spec = pl.BlockSpec((rows, kv_width), lambda g, *_: (0, 0))
    outs = pl.pallas_call(
        functools.partial(attention_kernel, order),
        grid_spec=pltpu.PrefetchScalarGridSpec(
            num_scalar_prefetch=2,
            grid=(width // pair,),
            in_specs=[row_spec, row_spec] + [kv_spec] * 4,
            out_specs=[row_spec] + [kv_spec] * 4,
            scratch_shapes=[
                pltpu.VMEM((4 * rows, 2 * tok), F32),
                pltpu.VMEM((4 * rows, 2 * tok), F32),
                pltpu.VMEM((head_dim, 4 * rows), BF16),
                pltpu.VMEM((4 * rows, kv_width), F32),
            ],
        ),
        out_shape=[jax.ShapeDtypeStruct((tok, width), BF16)]
        + [jax.ShapeDtypeStruct((rows, kv_width), BF16)] * 4,
        compiler_params=pltpu.CompilerParams(vmem_limit_bytes=16 << 20),
        cost_estimate=pl.CostEstimate(
            flops=flops, bytes_accessed=4 * 2 * rows * kv_width * 2, transcendentals=0
        ),
        name="attention",
    )(me, blocks, q, o, *kv_parts)
    return outs[0], list(outs[1:])


def grad_kernel(halves, slots, slab_ref, *refs):
    x_refs, refs = refs[:slots], list(refs[slots:])
    out_ref, xs_ref = refs[-2:]
    dq_refs = []
    for count in halves:
        dq_refs.append(refs[:count])
        del refs[:count]
    dkv_refs = refs[: len(halves)]
    acc_refs = refs[len(halves) : -2]
    own = xs_ref.shape[0]
    tok = x_refs[0].shape[1]
    rows, tile = dkv_refs[0].shape
    rows_at = pl.ds(pl.multiple_of(slab_ref[0] * own, own), own)
    for i, x_ref in enumerate(x_refs):
        xs_ref[:, i * tok : (i + 1) * tok] = x_ref[rows_at, :]

    def put(parts, columns):
        out = None
        for j, part in enumerate(parts):
            term = jnp.dot(xs_ref[:, j * rows : (j + 1) * rows], part, preferred_element_type=F32)
            out = term if out is None else out + term
        for ref in acc_refs:
            out = out + ref[:, columns]
        out_ref[:, columns] = out.astype(out_ref.dtype)

    def run(side, first, count):
        def step(t, _):
            to = pl.multiple_of(first + t * tile, tile)
            parts = []
            for pair in dq_refs:
                split = len(pair) == 2
                at = pl.multiple_of(t * tile, tile) if split else to
                parts.append(pair[side if split else 0][:, pl.ds(at, tile)])
            put(parts, pl.ds(to, tile))
            return 0

        lax.fori_loop(0, count, step, 0, unroll=True)

    half = (out_ref.shape[1] - tile) // 2
    run(0, 0, half // tile)
    run(1, half, half // tile)
    put([ref[...] for ref in dkv_refs], pl.ds(2 * half, tile))


def grad_call(groups, slab, kind, acc=()):
    xs = [block for group in groups for block in group[0]]
    dqs = [group[1] if isinstance(group[1], tuple) else (group[1],) for group in groups]
    dkvs = [group[2] for group in groups]
    tok = xs[0].shape[1]
    own = xs[0].shape[0] // lax.axis_size("dp")
    width = sum(half.shape[1] for half in dqs[0]) + dkvs[0].shape[1]
    operands = xs + [half for halves in dqs for half in halves] + dkvs + list(acc)
    in_place = pl.BlockSpec(memory_space=pltpu.VMEM)
    return pl.pallas_call(
        functools.partial(grad_kernel, [len(halves) for halves in dqs], len(xs)),
        in_specs=[pl.BlockSpec(memory_space=pltpu.SMEM)] + [in_place] * len(operands),
        out_specs=in_place,
        out_shape=jax.ShapeDtypeStruct((own, width), kind),
        scratch_shapes=[pltpu.VMEM((own, len(xs) * tok), BF16)],
        compiler_params=pltpu.CompilerParams(vmem_limit_bytes=16 << 20),
        cost_estimate=pl.CostEstimate(
            flops=2 * len(xs) * tok * own * width,
            bytes_accessed=sum(x.size * x.dtype.itemsize for x in operands),
            transcendentals=0,
        ),
        name="weight_grad",
    )(slab, *operands)


def update_kernel(others, tile, grad_ref, *refs):
    other_refs, state = refs[:others], refs[others : others + 3]
    outs, held, sem = refs[others + 3 : others + 6], refs[others + 6 : others + 9], refs[-1]
    inv_one = 1.0 / (1.0 - BETA_ONE**STEP)
    inv_two = 1.0 / (1.0 - BETA_TWO**STEP)

    def step(t, _):
        columns = pl.ds(pl.multiple_of(t * tile, tile), tile)
        grad = grad_ref[:, columns]
        for ref in other_refs:
            grad = grad + ref[:, columns].astype(F32)
        master, one, two = (ref[:, columns] for ref in state)
        new_one = BETA_ONE * one + (1.0 - BETA_ONE) * grad
        new_two = BETA_TWO * two + (1.0 - BETA_TWO) * grad * grad
        update = (new_one * inv_one) / (jnp.sqrt(new_two * inv_two) + EPSILON)
        held[0][:, columns] = master - LEARN_RATE * (update + DECAY * master)
        held[1][:, columns] = new_one
        held[2][:, columns] = new_two
        for i in range(3):
            pltpu.make_async_copy(
                held[i].at[:, columns], outs[i].at[:, columns], sem.at[i]
            ).start()
        return 0

    lax.fori_loop(0, grad_ref.shape[1] // tile, step, 0)
    for i in range(3):
        pltpu.make_async_copy(held[i], outs[i], sem.at[i]).wait()


def update_call(grad, others, state, tile):
    in_place = pl.BlockSpec(memory_space=pltpu.VMEM)
    return pl.pallas_call(
        functools.partial(update_kernel, len(others), tile),
        in_specs=[in_place] * (4 + len(others)),
        out_specs=[pl.BlockSpec(memory_space=pl.ANY)] * 3,
        out_shape=[jax.ShapeDtypeStruct(grad.shape, F32)] * 3,
        scratch_shapes=[pltpu.VMEM(grad.shape, F32)] * 3 + [pltpu.SemaphoreType.DMA((3,))],
        compiler_params=pltpu.CompilerParams(vmem_limit_bytes=16 << 20),
        cost_estimate=pl.CostEstimate(
            flops=20 * grad.size, bytes_accessed=28 * grad.size, transcendentals=grad.size
        ),
        name="weight_update",
    )(grad, *others, *state)


def per_device(
    layer_input,
    query_rows,
    key_rows,
    value_rows,
    out_grad,
    block_order,
    master,
    moment_one,
    moment_two,
):
    dp_count = lax.axis_size("dp")
    ctx_count = lax.axis_size("ctx")
    own_rows = master.shape[0]
    order = slot_order(ctx_count)
    me = lax.axis_index("ctx").astype(jnp.int32).reshape(1)
    dp_rank = lax.axis_index("dp").astype(jnp.int32)

    x_groups = []
    for j in range(4):
        masks = tuple(o ^ j for o in order)
        packed = pack(layer_input[0], me, masks, dp_count, ctx_count, own_rows)
        blocks = []
        for i, o in enumerate(order):
            block = packed[i]
            blocks.append(block if o ^ j == 0 else swap(block, o ^ j, ctx_count))
        x_groups.append(blocks)

    kv_parts = spread(jnp.concatenate([key_rows[0], value_rows[0]], axis=1), ctx_count)
    dq, dkv_terms = attention(me, block_order, query_rows[0], out_grad[0], kv_parts, order)
    dq_parts = spread(dq, ctx_count, relay=True)
    dkv_parts = fan_out(total_terms(dkv_terms, ctx_count), ctx_count)
    groups = list(zip(x_groups, dq_parts, dkv_parts))

    slabs = [lax.rem(dp_rank + k, dp_count).reshape(1) for k in range(dp_count)]
    most = []
    for k in range(dp_count):
        most.append(grad_call(groups[:3], slabs[k], F32))
    received = []
    for k in range(1, dp_count):
        part = grad_call(groups[3:], slabs[k], BF16, most[k : k + 1])
        received.append(
            lax.ppermute(part, "dp", [(i, (i + k) % dp_count) for i in range(dp_count)])
        )
    grad = grad_call(groups[3:], slabs[0], F32, most[:1])
    state = (master, moment_one, moment_two)
    return tuple(update_call(grad, received, state, 2 * key_rows.shape[2]))


def solution(mesh):
    in_specs = (
        P("dp", "ctx", None),
        P("dp", "ctx", None),
        P("dp", "ctx", None),
        P("dp", "ctx", None),
        P("dp", "ctx", None),
        P(),
        P(("dp", "ctx"), None),
        P(("dp", "ctx"), None),
        P(("dp", "ctx"), None),
    )
    out_specs = (P(("dp", "ctx"), None), P(("dp", "ctx"), None), P(("dp", "ctx"), None))

    return jax.shard_map(
        per_device, mesh=mesh, in_specs=in_specs, out_specs=out_specs, check_vma=False
    )
```

```python
import functools
import math

import jax
import jax.numpy as jnp
from jax import lax
from jax.experimental import pallas as pl
from jax.experimental.pallas import tpu as pltpu
from jax.sharding import PartitionSpec as P


STEP = 10
BETA_ONE = 0.9
BETA_TWO = 0.95
EPSILON = 1e-08
LEARN_RATE = 0.01
DECAY = 0.1
NEG_FILL = -1e30
LOG2E = 1.4426950408889634
ROW_CONTRACT = (((1,), (1,)), ((), ()))
F32 = jnp.float32
BF16 = jnp.bfloat16


def swap(block, mask, count):
    return lax.ppermute(block, "ctx", [(i, i ^ mask) for i in range(count)])


def stage_bits(count):
    bits = []
    bit = count // 2
    while bit >= 4:
        bits.append(bit)
        bit //= 2
    return bits


def slot_order(count):
    order = [0]
    for bit in stage_bits(count):
        order = order + [o ^ bit for o in order]
    return order


def fan_out(held, count, relay=False):
    parts = [held] + [swap(held, j, count) for j in range(1, 3)]
    if not relay:
        return parts + [swap(held, 3, count)]
    half = held.shape[1] // 2
    left = swap(parts[1][:, :half], 2, count)
    right = swap(parts[2][:, half:], 1, count)
    return parts + [(left, right)]


def spread(block, count, relay=False):
    held = block
    for bit in stage_bits(count):
        held = jnp.concatenate([held, swap(held, bit, count)], axis=0)
    return fan_out(held, count, relay)


def total_terms(parts, count):
    total = parts[0].astype(F32)
    for j in range(1, 4):
        other = swap(parts[j], j, count)
        total = total + other.astype(F32)
    tok = total.shape[0] // (count // 4)
    order = slot_order(count)
    for bit in stage_bits(count):
        other = swap(total.astype(BF16), bit, count)
        blocks = [other[order.index(o ^ bit) * tok :][:tok] for o in order]
        total = total + jnp.concatenate(blocks, axis=0).astype(F32)
    return total.astype(BF16)


def pack_kernel(masks, dp_count, ctx_count, me_ref, x_ref, *refs):
    outs = refs[: len(masks)]
    held_ref, sem = refs[len(masks) :]
    own = held_ref.shape[2]
    copies = []
    for i, mask in enumerate(masks):
        for d in range(dp_count):
            first = pl.multiple_of((d * ctx_count + (me_ref[0] ^ mask)) * own, 128)
            at = i * dp_count + d
            copies.append(
                pltpu.make_async_copy(
                    x_ref.at[:, pl.ds(first, own)], held_ref.at[at], sem.at[at]
                )
            )
    for copy in copies:
        copy.start()
    for i, out_ref in enumerate(outs):
        for d in range(dp_count):
            at = i * dp_count + d
            copies[at].wait()
            out_ref[d * own : (d + 1) * own, :] = held_ref[at].T


def pack(rows, me, masks, dp_count, ctx_count, own):
    tok = rows.shape[0]
    count = len(masks)
    if own % 128:
        slabs = rows.T.reshape(dp_count, ctx_count, own, tok).transpose(1, 0, 2, 3)
        slabs = slabs.reshape(ctx_count, dp_count * own, tok)
        return [lax.dynamic_index_in_dim(slabs, me[0] ^ mask, 0, False) for mask in masks]
    return pl.pallas_call(
        functools.partial(pack_kernel, masks, dp_count, ctx_count),
        in_specs=[
            pl.BlockSpec(memory_space=pltpu.SMEM),
            pl.BlockSpec(memory_space=pltpu.HBM),
        ],
        out_specs=[pl.BlockSpec(memory_space=pltpu.VMEM)] * count,
        out_shape=[jax.ShapeDtypeStruct((dp_count * own, tok), rows.dtype)] * count,
        scratch_shapes=[
            pltpu.VMEM((count * dp_count, tok, own), rows.dtype),
            pltpu.SemaphoreType.DMA((count * dp_count,)),
        ],
        compiler_params=pltpu.CompilerParams(vmem_limit_bytes=8 << 20),
        cost_estimate=pl.CostEstimate(
            flops=0, bytes_accessed=4 * count * dp_count * own * tok, transcendentals=0
        ),
        name="pack_rows",
    )(me, pltpu.with_memory_space_constraint(rows, pltpu.HBM))


def attention_kernel(order, me_ref, blocks_ref, q_ref, o_ref, *refs):
    kv_refs = refs[:4]
    dq_ref = refs[4]
    dkv_refs = refs[5:9]
    s_ref, g_ref, kt_ref, acc_ref = refs[9:]
    step = pl.program_id(0)
    tok, pair = q_ref.shape
    head_dim = pair // 2
    half = tok // 2
    rows = kv_refs[0].shape[0]
    me = me_ref[0]
    scale = 1.0 / math.sqrt(head_dim)

    @pl.when(step == 0)
    def _():
        acc_ref[...] = jnp.zeros_like(acc_ref)
        for j in range(4):
            kt_ref[:, j * rows : (j + 1) * rows] = kv_refs[j][:, :head_dim].T

    q2 = jnp.concatenate([q_ref[:, :head_dim], q_ref[:, head_dim:]], axis=0)
    o2 = jnp.concatenate([o_ref[:, :head_dim], o_ref[:, head_dim:]], axis=0)
    lane = lax.broadcasted_iota(jnp.int32, (1, 2 * tok), 1)
    lane = jnp.where(lane >= tok, lane - tok, lane)
    first = blocks_ref[2 * me]
    second = blocks_ref[2 * me + 1]
    query_pos = jnp.where(lane < half, first * half + lane, second * half + lane - half)
    in_block = lax.broadcasted_iota(jnp.int32, (half, 2 * tok), 0)

    top = jnp.full((1, 2 * tok), NEG_FILL, F32)
    for j in range(4):
        scores = lax.dot_general(
            kv_refs[j][:, :head_dim], q2, ROW_CONTRACT, preferred_element_type=F32
        )
        for i, o in enumerate(order):
            for u in range(2):
                lo = i * tok + u * half
                key_base = blocks_ref[2 * (me ^ (o ^ j)) + u] * half
                part = scores[lo : lo + half] * (scale * LOG2E)
                part = jnp.where(in_block <= query_pos - key_base, part, NEG_FILL)
                s_ref[j * rows + lo : j * rows + lo + half, :] = part
                top = jnp.maximum(top, jnp.max(part, axis=0, keepdims=True))
    denom = jnp.zeros((1, 2 * tok), F32)
    inner = jnp.zeros((1, 2 * tok), F32)
    for j in range(4):
        grads = lax.dot_general(
            kv_refs[j][:, head_dim:], o2, ROW_CONTRACT, preferred_element_type=F32
        )
        g_ref[j * rows : (j + 1) * rows, :] = grads
        for lo in range(0, rows, half):
            at = slice(j * rows + lo, j * rows + lo + half)
            weight = jnp.exp2(s_ref[at, :] - top)
            s_ref[at, :] = weight
            denom = denom + jnp.sum(weight, axis=0, keepdims=True)
            inner = inner + jnp.sum(weight * grads[lo : lo + half], axis=0, keepdims=True)
    inv = 1.0 / denom
    delta = inner * inv
    dqt = jnp.zeros((head_dim, 2 * tok), F32)
    for j in range(4):
        at = slice(j * rows, (j + 1) * rows)
        prob = s_ref[at, :] * inv
        ds = (prob * (g_ref[at, :] - delta) * scale).astype(BF16)
        prob = prob.astype(BF16)
        acc_ref[at, :head_dim] += jnp.dot(ds, q2, preferred_element_type=F32)
        acc_ref[at, head_dim:] += jnp.dot(prob, o2, preferred_element_type=F32)
        dqt = dqt + jnp.dot(kt_ref[:, at], ds, preferred_element_type=F32)
    dq2 = dqt.T.astype(BF16)
    dq_ref[:, :head_dim] = dq2[:tok]
    dq_ref[:, head_dim:] = dq2[tok:]

    @pl.when(step == pl.num_programs(0) - 1)
    def _():
        for j in range(4):
            dkv_refs[j][...] = acc_ref[j * rows : (j + 1) * rows, :].astype(BF16)


def attention(me, blocks, q, o, kv_parts, order):
    tok, width = q.shape
    rows, kv_width = kv_parts[0].shape
    head_dim = kv_width // 2
    pair = 2 * head_dim
    flops = 2 * 5 * tok * (width // head_dim) * 4 * rows * head_dim
    row_spec = pl.BlockSpec((tok, pair), lambda g, *_: (0, g))
    kv_spec = pl.BlockSpec((rows, kv_width), lambda g, *_: (0, 0))
    outs = pl.pallas_call(
        functools.partial(attention_kernel, order),
        grid_spec=pltpu.PrefetchScalarGridSpec(
            num_scalar_prefetch=2,
            grid=(width // pair,),
            in_specs=[row_spec, row_spec] + [kv_spec] * 4,
            out_specs=[row_spec] + [kv_spec] * 4,
            scratch_shapes=[
                pltpu.VMEM((4 * rows, 2 * tok), F32),
                pltpu.VMEM((4 * rows, 2 * tok), F32),
                pltpu.VMEM((head_dim, 4 * rows), BF16),
                pltpu.VMEM((4 * rows, kv_width), F32),
            ],
        ),
        out_shape=[jax.ShapeDtypeStruct((tok, width), BF16)]
        + [jax.ShapeDtypeStruct((rows, kv_width), BF16)] * 4,
        compiler_params=pltpu.CompilerParams(vmem_limit_bytes=16 << 20),
        cost_estimate=pl.CostEstimate(
            flops=flops, bytes_accessed=4 * 2 * rows * kv_width * 2, transcendentals=0
        ),
        name="attention",
    )(me, blocks, q, o, *kv_parts)
    return outs[0], list(outs[1:])


def grad_kernel(halves, slots, slab_ref, *refs):
    x_refs, refs = refs[:slots], list(refs[slots:])
    out_ref, xs_ref = refs[-2:]
    dq_refs = []
    for count in halves:
        dq_refs.append(refs[:count])
        del refs[:count]
    dkv_refs = refs[: len(halves)]
    acc_refs = refs[len(halves) : -2]
    own = xs_ref.shape[0]
    tok = x_refs[0].shape[1]
    rows, tile = dkv_refs[0].shape
    rows_at = pl.ds(pl.multiple_of(slab_ref[0] * own, own), own)
    for i, x_ref in enumerate(x_refs):
        xs_ref[:, i * tok : (i + 1) * tok] = x_ref[rows_at, :]

    def put(parts, columns):
        out = None
        for j, part in enumerate(parts):
            term = jnp.dot(xs_ref[:, j * rows : (j + 1) * rows], part, preferred_element_type=F32)
            out = term if out is None else out + term
        for ref in acc_refs:
            out = out + ref[:, columns]
        out_ref[:, columns] = out.astype(out_ref.dtype)

    def run(side, first, count):
        def step(t, _):
            to = pl.multiple_of(first + t * tile, tile)
            parts = []
            for pair in dq_refs:
                split = len(pair) == 2
                at = pl.multiple_of(t * tile, tile) if split else to
                parts.append(pair[side if split else 0][:, pl.ds(at, tile)])
            put(parts, pl.ds(to, tile))
            return 0

        lax.fori_loop(0, count, step, 0, unroll=True)

    half = (out_ref.shape[1] - tile) // 2
    run(0, 0, half // tile)
    run(1, half, half // tile)
    put([ref[...] for ref in dkv_refs], pl.ds(2 * half, tile))


def grad_call(groups, slab, kind, acc=()):
    xs = [block for group in groups for block in group[0]]
    dqs = [group[1] if isinstance(group[1], tuple) else (group[1],) for group in groups]
    dkvs = [group[2] for group in groups]
    tok = xs[0].shape[1]
    own = xs[0].shape[0] // lax.axis_size("dp")
    width = sum(half.shape[1] for half in dqs[0]) + dkvs[0].shape[1]
    operands = xs + [half for halves in dqs for half in halves] + dkvs + list(acc)
    in_place = pl.BlockSpec(memory_space=pltpu.VMEM)
    return pl.pallas_call(
        functools.partial(grad_kernel, [len(halves) for halves in dqs], len(xs)),
        in_specs=[pl.BlockSpec(memory_space=pltpu.SMEM)] + [in_place] * len(operands),
        out_specs=in_place,
        out_shape=jax.ShapeDtypeStruct((own, width), kind),
        scratch_shapes=[pltpu.VMEM((own, len(xs) * tok), BF16)],
        compiler_params=pltpu.CompilerParams(vmem_limit_bytes=16 << 20),
        cost_estimate=pl.CostEstimate(
            flops=2 * len(xs) * tok * own * width,
            bytes_accessed=sum(x.size * x.dtype.itemsize for x in operands),
            transcendentals=0,
        ),
        name="weight_grad",
    )(slab, *operands)


def update_kernel(others, tile, grad_ref, *refs):
    other_refs, state = refs[:others], refs[others : others + 3]
    outs, held, sem = refs[others + 3 : others + 6], refs[others + 6 : others + 9], refs[-1]
    inv_one = 1.0 / (1.0 - BETA_ONE**STEP)
    inv_two = 1.0 / (1.0 - BETA_TWO**STEP)

    def step(t, _):
        columns = pl.ds(pl.multiple_of(t * tile, tile), tile)
        grad = grad_ref[:, columns]
        for ref in other_refs:
            grad = grad + ref[:, columns].astype(F32)
        master, one, two = (ref[:, columns] for ref in state)
        new_one = BETA_ONE * one + (1.0 - BETA_ONE) * grad
        new_two = BETA_TWO * two + (1.0 - BETA_TWO) * grad * grad
        update = (new_one * inv_one) / (jnp.sqrt(new_two * inv_two) + EPSILON)
        held[0][:, columns] = master - LEARN_RATE * (update + DECAY * master)
        held[1][:, columns] = new_one
        held[2][:, columns] = new_two
        for i in range(3):
            pltpu.make_async_copy(
                held[i].at[:, columns], outs[i].at[:, columns], sem.at[i]
            ).start()
        return 0

    lax.fori_loop(0, grad_ref.shape[1] // tile, step, 0)
    for i in range(3):
        pltpu.make_async_copy(held[i], outs[i], sem.at[i]).wait()


def update_call(grad, others, state, tile):
    in_place = pl.BlockSpec(memory_space=pltpu.VMEM)
    return pl.pallas_call(
        functools.partial(update_kernel, len(others), tile),
        in_specs=[in_place] * (4 + len(others)),
        out_specs=[pl.BlockSpec(memory_space=pl.ANY)] * 3,
        out_shape=[jax.ShapeDtypeStruct(grad.shape, F32)] * 3,
        scratch_shapes=[pltpu.VMEM(grad.shape, F32)] * 3 + [pltpu.SemaphoreType.DMA((3,))],
        compiler_params=pltpu.CompilerParams(vmem_limit_bytes=16 << 20),
        cost_estimate=pl.CostEstimate(
            flops=20 * grad.size, bytes_accessed=28 * grad.size, transcendentals=grad.size
        ),
        name="weight_update",
    )(grad, *others, *state)


def per_device(
    layer_input,
    query_rows,
    key_rows,
    value_rows,
    out_grad,
    block_order,
    master,
    moment_one,
    moment_two,
):
    dp_count = lax.axis_size("dp")
    ctx_count = lax.axis_size("ctx")
    own_rows = master.shape[0]
    order = slot_order(ctx_count)
    me = lax.axis_index("ctx").astype(jnp.int32).reshape(1)
    dp_rank = lax.axis_index("dp").astype(jnp.int32)

    blocks = {}
    for j in range(4):
        masks = tuple(o ^ j for o in order if o ^ j) + (0,) * (j == 3)
        packed = pack(layer_input[0], me, masks, dp_count, ctx_count, own_rows)
        for mask, block in zip(masks, packed):
            blocks[mask] = swap(block, mask, ctx_count) if mask else block
    x_groups = [[blocks[o ^ j] for o in order] for j in range(4)]

    kv_parts = spread(jnp.concatenate([key_rows[0], value_rows[0]], axis=1), ctx_count)
    dq, dkv_terms = attention(me, block_order, query_rows[0], out_grad[0], kv_parts, order)
    dq_parts = spread(dq, ctx_count, relay=True)
    dkv_parts = fan_out(total_terms(dkv_terms, ctx_count), ctx_count)
    groups = list(zip(x_groups, dq_parts, dkv_parts))

    slabs = [lax.rem(dp_rank + k, dp_count).reshape(1) for k in range(dp_count)]
    most = []
    for k in range(dp_count):
        most.append(grad_call(groups[:3], slabs[k], F32))
    received = []
    for k in range(1, dp_count):
        part = grad_call(groups[3:], slabs[k], BF16, most[k : k + 1])
        received.append(
            lax.ppermute(part, "dp", [(i, (i + k) % dp_count) for i in range(dp_count)])
        )
    grad = grad_call(groups[3:], slabs[0], F32, most[:1])
    state = (master, moment_one, moment_two)
    return tuple(update_call(grad, received, state, 2 * key_rows.shape[2]))


def solution(mesh):
    in_specs = (
        P("dp", "ctx", None),
        P("dp", "ctx", None),
        P("dp", "ctx", None),
        P("dp", "ctx", None),
        P("dp", "ctx", None),
        P(),
        P(("dp", "ctx"), None),
        P(("dp", "ctx"), None),
        P(("dp", "ctx"), None),
    )
    out_specs = (P(("dp", "ctx"), None), P(("dp", "ctx"), None), P(("dp", "ctx"), None))

    return jax.shard_map(
        per_device, mesh=mesh, in_specs=in_specs, out_specs=out_specs, check_vma=False
    )
```
